32 devices in a mesh: section: 2 (over x), dp: 16 (over z, y, core).
Axes of the slice: x: 2, y: 2, z: 4, core: 2. Of those that a mesh axis runs over, the one named last changes fastest.
Arguments:
- text: bfloat16 [3072, 8192], P('dp'), may hold values from -60 to 60
- image: bfloat16 [768, 3200], P('dp'), may hold values from -60 to 60
- positions: int32 [48, 16], P('dp'), may hold values from 0 to 63, as said below
- enc_in: bfloat16 [2, 3200, 128], P('section', 'dp'), may hold values from -0.109375 to 0.109375
- enc_out: bfloat16 [2, 128, 3200], P('section', None, 'dp'), may hold values from -0.5 to 0.5
- conn_in: bfloat16 [3200, 64], P('dp'), may hold values from -0.109375 to 0.109375
- conn_out: bfloat16 [64, 8192], P(None, 'dp'), may hold values from -0.75 to 0.75
- llm_in: bfloat16 [2, 8192, 512], P('section', 'dp'), may hold values from -0.0625 to 0.0625
- llm_out: bfloat16 [2, 512, 8192], P('section', None, 'dp'), may hold values from -0.25 to 0.25
Outputs:
- layer_states: bfloat16 [2, 3072, 8192], P('section', 'dp')
The draws below stay inside these ranges and needn't reach their ends.
Inputs may be any that keep to these rules, and one draw needn't show every extreme that they name: Each row holds 16 distinct positions within one micro-batch of 64 rows, in ascending order.
All inputs are finite; a program needn't handle non-finite values.
Results may differ from the reference program's by a relative error of at most 0.009.
Values may be sent and summed in bfloat16 or wider, within the bound.
No kernel may reach another device: no remote copies, remote signals or barrier semaphores. Data moves between devices by JAX's collectives and lax.ppermute only.
A program may use at most 128 MiB of HBM per device.

```python
import math
import jax
import jax.numpy as jnp
from jax import lax

D = 8192
DV = 3200
RANK = 512
ENC_RANK = 128
CONN_RANK = 64
ROWS = 64
IMG = 16
LAYER_COUNT = 2
MB_ALL = 48
TEXT_ROWS = 3072
IMG_ROWS = 768


def scaled_field(key, row_count, col_count):
    first, second, third = jax.random.split(key, 3)
    base = jnp.clip(jax.random.normal(first, (row_count, col_count), jnp.float32), -4.0, 4.0)
    per_row_scale = jnp.exp(jax.random.uniform(second, (row_count, 1), jnp.float32, math.log(0.3), math.log(3.0)))
    col_scale = jnp.exp(jax.random.uniform(third, (1, col_count), jnp.float32, math.log(0.5), math.log(5.0)))
    return (base * per_row_scale * col_scale).astype(jnp.bfloat16)


def draw_text(key, part):
    return scaled_field(jax.random.fold_in(key, 11), TEXT_ROWS, D)


def draw_image(key, part):
    return scaled_field(jax.random.fold_in(key, 23), IMG_ROWS, DV)


def draw_positions(key, part):
    row_keys = jax.random.split(jax.random.fold_in(key, 37), MB_ALL)

    def one_row(random_row_key):
        shuffled = jax.random.permutation(random_row_key, ROWS)
        return jnp.sort(shuffled[:IMG]).astype(jnp.int32)
    return jax.vmap(one_row)(row_keys)


def shard_levels(stream_key, extent, cuts, low, top_value):
    level, own = 1.0, jax.random.fold_in(stream_key, 6)
    for position, blocks in cuts:
        heights = jnp.exp(jax.random.uniform(jax.random.fold_in(own, position), (blocks,), jnp.float32, low / len(cuts), top_value / len(cuts)))
        level = level * jnp.repeat(heights, extent[position] // blocks).reshape([-1 if axis == position else 1 for axis in range(len(extent))])
    return level


def normal_values(rng, extent, spread, limit, cuts=(), kind=jnp.bfloat16):
    result = spread * jax.random.normal(rng, extent, jnp.float32)
    if cuts:
        result = result * shard_levels(rng, extent, cuts, -0.22, 0.18)
    return jnp.clip(result, -limit, limit).astype(kind)


def setup_inputs(seed: int = 0) -> dict:
    splits = jax.random.split(jax.random.key(seed), 10)
    return {
        "text": draw_text(jax.random.fold_in(splits[9], 71), 0),
        "image": draw_image(jax.random.fold_in(splits[9], 71), 0),
        "positions": draw_positions(jax.random.fold_in(splits[9], 71), 0),
        "enc_in": normal_values(splits[3], (LAYER_COUNT, DV, ENC_RANK), DV ** -0.5, 0.109375, ((0, 2), (1, 16))),
        "enc_out": normal_values(splits[4], (LAYER_COUNT, ENC_RANK, DV), ENC_RANK ** -0.5, 0.5, ((0, 2), (2, 16))),
        "conn_in": normal_values(splits[5], (DV, CONN_RANK), DV ** -0.5, 0.109375, ((0, 16),)),
        "conn_out": normal_values(splits[6], (CONN_RANK, D), CONN_RANK ** -0.5, 0.75, ((1, 16),)),
        "llm_in": normal_values(splits[7], (LAYER_COUNT, D, RANK), D ** -0.5, 0.0625, ((0, 2), (1, 16))),
        "llm_out": normal_values(splits[8], (LAYER_COUNT, RANK, D), RANK ** -0.5, 0.25, ((0, 2), (2, 16))),
    }


EPSILON = 1e-06

def normed_rows(expanded_rows):
    scale = lax.rsqrt(lax.optimization_barrier(jnp.mean(expanded_rows * expanded_rows, axis=-1, keepdims=True)) + EPSILON)
    return (expanded_rows * scale).astype(jnp.bfloat16)

def encoder_act(values):
    return jax.nn.gelu(values, approximate=False)

def adapter_layer(hidden, weight_in, weight_out, nonlinear):
    expanded_rows = hidden.astype(jnp.float32)
    normed = normed_rows(expanded_rows)
    projected = jnp.dot(normed, weight_in, preferred_element_type=jnp.float32)
    activated = nonlinear(projected).astype(jnp.bfloat16)
    branch = jnp.dot(activated, weight_out, preferred_element_type=jnp.float32)
    return (expanded_rows + branch).astype(jnp.bfloat16)

def reference(text, image, positions, enc_in, enc_out, conn_in, conn_out, llm_in, llm_out):
    encoded = image
    for layer_index in range(LAYER_COUNT):
        encoded = adapter_layer(encoded, enc_in[layer_index], enc_out[layer_index], encoder_act)
    latent = encoder_act(jnp.dot(normed_rows(encoded.astype(jnp.float32)), conn_in, preferred_element_type=jnp.float32)).astype(jnp.bfloat16)
    picture_row_block = jnp.dot(latent, conn_out, preferred_element_type=jnp.float32).astype(jnp.bfloat16)
    picture_row_block = picture_row_block.reshape(MB_ALL, IMG, D)
    state = text.reshape(MB_ALL, ROWS, D)
    batch_index = jnp.broadcast_to(jnp.arange(MB_ALL, dtype=jnp.int32)[:, None], (MB_ALL, IMG))
    state = state.at[batch_index, positions.astype(jnp.int32)].set(picture_row_block)
    state = state.reshape(MB_ALL * ROWS, D)
    hidden_state_list = []
    for layer_index in range(LAYER_COUNT):
        state = adapter_layer(state, llm_in[layer_index], llm_out[layer_index], jax.nn.silu)
        hidden_state_list.append(state)
    return jnp.stack(hidden_state_list)
```

```python
import functools

import jax
import jax.numpy as jnp
import numpy as np
from jax import lax
from jax.experimental import pallas as pl
from jax.experimental.pallas import tpu as pltpu
from jax.sharding import PartitionSpec as P

EPSILON = 1e-06
BF16 = jnp.bfloat16
F32 = jnp.float32


def chip_cycle(mesh, count):
    plain = list(range(count))
    line = mesh.devices.reshape(-1, mesh.shape["dp"])[0][::2]
    coords = [tuple(getattr(dev, "coords", (i,))) for i, dev in enumerate(line)]
    if len(set(coords)) != count:
        return plain
    varying = [a for a in range(len(coords[0])) if len({c[a] for c in coords}) > 1]
    if len(varying) != 2:
        return plain
    first, second = varying
    if len({c[first] for c in coords}) % 2:
        first, second = second, first
    rows = sorted({c[first] for c in coords})
    cols = sorted({c[second] for c in coords})
    if len(rows) % 2 or len(rows) * len(cols) != count:
        return plain
    where = {(c[first], c[second]): i for i, c in enumerate(coords)}
    path = []
    for n, row in enumerate(rows):
        walk = cols[1:] if n % 2 == 0 else cols[:0:-1]
        path += [where[row, col] for col in walk]
    return path + [where[row, cols[0]] for row in reversed(rows)]


class Ring:
    def __init__(self, cycle):
        self.cycle = cycle
        self.chips = len(cycle)
        self.reach = self.chips // 2
        self.place = {chip: i for i, chip in enumerate(cycle)}
        self.groups = [[0, 1]]
        used = 2
        for k in range(1, self.reach + 1):
            size = 2 if 2 * k == self.chips else 4
            self.groups.append(list(range(used, used + size)))
            used += size
        self.slots = used
        self.table = np.array([self.sources(d) for d in range(2 * self.chips)], np.int32)

    def sources(self, device):
        chip, core = divmod(device, 2)
        at = self.place[chip]
        found = [device, device ^ 1]
        for k in range(1, self.reach + 1):
            hops = (-k,) if 2 * k == self.chips else (-k, k)
            for hop in hops:
                other = self.cycle[(at + hop) % self.chips]
                found += [2 * other + core, 2 * other + 1 - core]
        return found

    def shift(self, x, by):
        pairs = []
        for i, chip in enumerate(self.cycle):
            to = self.cycle[(i + by) % self.chips]
            pairs += [(2 * chip + core, 2 * to + core) for core in (0, 1)]
        return lax.ppermute(x, "dp", pairs)

    def swap(self, x):
        return lax.ppermute(x, "dp", [(i, i ^ 1) for i in range(2 * self.chips)])

    def gather(self, first, second, after=None):
        if after is not None:
            first, second, _ = lax.optimization_barrier((first, second, after))
        got = [[None] * self.slots, [None] * self.slots]
        token = first
        for part, own in enumerate((first, second)):
            got[part][0], got[part][1] = own, self.swap(own)
        ahead, behind = [first, second], [first, second]
        for k in range(1, self.reach + 1):
            group = self.groups[k]
            token = (ahead[0], behind[1])
            far = 2 * k == self.chips
            for part in (0, 1):
                if not far or part == 0:
                    ahead[part] = self.shift(ahead[part], 1)
                if not far or part == 1:
                    behind[part] = self.shift(behind[part], -1)
            for part in (0, 1):
                arrived = [ahead[part], behind[part]]
                if far:
                    arrived = [arrived[part]]
                for n, x in enumerate(arrived):
                    got[part][group[2 * n]] = x
                    got[part][group[2 * n + 1]] = self.swap(x)
        return got, token


def whole(x):
    return pl.BlockSpec(x.shape, lambda *_: (0,) * x.ndim)


def gelu(values):
    return 0.5 * values * (1.0 + lax.erf(values * np.float32(np.sqrt(0.5))))


def encoder_kernel(slots, width, has_conn, *refs):
    hidden_ref = refs[0]
    packs = refs[1 : 1 + slots]
    conns = refs[1 + slots : 1 + slots + (slots if has_conn else 0)]
    out_ref = refs[-1]

    def scale_of(blocks):
        total = sum(jnp.sum(b * b, axis=-1, keepdims=True) for b in blocks)
        return lax.rsqrt(total / width + EPSILON)

    blocks = [hidden_ref[j].astype(F32) for j in range(slots)]
    scale = scale_of(blocks)
    total = sum(
        jnp.dot((b * scale).astype(BF16), packs[j][0], preferred_element_type=F32)
        for j, b in enumerate(blocks)
    )
    active = gelu(total).astype(BF16)
    contract = (((1,), (1,)), ((), ()))
    outs = [
        (b + lax.dot_general(active, packs[j][1], contract, preferred_element_type=F32)).astype(BF16)
        for j, b in enumerate(blocks)
    ]
    if not has_conn:
        for j in range(slots):
            out_ref[j] = outs[j]
        return
    blocks = [b.astype(F32) for b in outs]
    scale = scale_of(blocks)
    part = blocks[0].shape[-1]
    total = sum(
        lax.dot_general(
            (b * scale).astype(BF16), conns[j][:, :part], contract, preferred_element_type=F32
        )
        for j, b in enumerate(blocks)
    )
    out_ref[...] = gelu(total).astype(BF16)


def encoder_layer(hidden, packs, conns):
    slots, rows, part = hidden.shape
    shape = (rows, conns[0].shape[0]) if conns else hidden.shape
    args = [hidden, *packs, *conns]
    return pl.pallas_call(
        functools.partial(encoder_kernel, slots, slots * part, bool(conns)),
        out_shape=jax.ShapeDtypeStruct(shape, BF16),
        in_specs=[whole(x) for x in args],
        out_specs=pl.BlockSpec(shape, lambda *_: (0,) * len(shape)),
        grid=(1,),
    )(*args)


def merge_kernel(source_ref, text_ref, place_ref, latent_ref, conn_ref, out_ref, square_ref):
    picture = jnp.dot(latent_ref[...], conn_ref[0], preferred_element_type=F32).astype(BF16)
    place = place_ref[...]
    placed = jnp.dot(place, picture, preferred_element_type=F32)
    taken = jnp.sum(place.astype(F32), axis=-1, keepdims=True) > 0.5
    merged = jnp.where(taken, placed, text_ref[...].astype(F32))
    out_ref[0] = merged.astype(BF16)

    @pl.when(pl.program_id(0) == 0)
    def _():
        square_ref[...] = jnp.zeros_like(square_ref)

    square_ref[...] += jnp.sum(merged * merged, axis=-1, keepdims=True)


def merge(sources, text, place, latent, conn_up):
    slots, inner, part = conn_up.shape
    rows = text.shape[0]
    return pl.pallas_call(
        merge_kernel,
        out_shape=(
            jax.ShapeDtypeStruct((slots, rows, part), BF16),
            jax.ShapeDtypeStruct((rows, 1), F32),
        ),
        grid_spec=pltpu.PrefetchScalarGridSpec(
            num_scalar_prefetch=1,
            grid=(slots,),
            in_specs=[
                pl.BlockSpec((rows, part), lambda j, s: (0, s[j])),
                pl.BlockSpec(place.shape, lambda j, s: (0, 0)),
                pl.BlockSpec(latent.shape, lambda j, s: (0, 0)),
                pl.BlockSpec((1, inner, part), lambda j, s: (j, 0, 0)),
            ],
            out_specs=(
                pl.BlockSpec((1, rows, part), lambda j, s: (j, 0, 0)),
                pl.BlockSpec((rows, 1), lambda j, s: (0, 0)),
            ),
        ),
    )(sources, text, place, latent, conn_up)


def down_kernel(count, has_total, *refs):
    blocks, firsts, seconds = refs[:count], refs[count : 2 * count], refs[2 * count : 3 * count]
    out_ref = refs[-1]
    half = firsts[0].shape[0]
    total = refs[3 * count][...] if has_total else jnp.zeros(out_ref.shape, F32)
    for x, a, b in zip(blocks, firsts, seconds):
        total += jnp.dot(x[0, :, :half], a[...], preferred_element_type=F32)
        total += jnp.dot(x[0, :, half:], b[...], preferred_element_type=F32)
    out_ref[...] = total


def down(total, state, group, firsts, seconds):
    _, rows, part = state.shape
    inner = firsts[0].shape[1]
    args = [state] * len(group) + firsts + seconds + ([] if total is None else [total])
    specs = [pl.BlockSpec((1, rows, part), lambda _, j=j: (j, 0, 0)) for j in group]
    return pl.pallas_call(
        functools.partial(down_kernel, len(group), total is not None),
        out_shape=jax.ShapeDtypeStruct((rows, inner), F32),
        in_specs=specs + [whole(x) for x in args[len(group) :]],
        out_specs=pl.BlockSpec((rows, inner), lambda *_: (0, 0)),
        grid=(1,),
    )(*args)


def up_half_kernel(count, section_ref, active_ref, *refs):
    blocks, firsts, seconds = refs[:count], refs[count : 2 * count], refs[2 * count : 3 * count]
    out_ref = refs[-1]
    half = firsts[0].shape[0]
    for n, (x, a, b) in enumerate(zip(blocks, firsts, seconds)):
        branch = jnp.dot(active_ref[:, :half], a[...], preferred_element_type=F32)
        branch += jnp.dot(active_ref[:, half:], b[...], preferred_element_type=F32)
        out_ref[n] = (x[0].astype(F32) + branch).astype(BF16)


def up_half(side, active, state, group, firsts, seconds):
    rows = state.shape[1]
    part = firsts[0].shape[1]
    args = [active] + [state] * len(group) + firsts + seconds
    specs = [pl.BlockSpec((1, rows, part), lambda _, s, j=j: (j, 0, s[0])) for j in group]
    return pl.pallas_call(
        functools.partial(up_half_kernel, len(group)),
        out_shape=jax.ShapeDtypeStruct((len(group), rows, part), BF16),
        grid_spec=pltpu.PrefetchScalarGridSpec(
            num_scalar_prefetch=1,
            grid=(1,),
            in_specs=[whole(active)] + specs + [whole(x) for x in firsts + seconds],
            out_specs=pl.BlockSpec((len(group), rows, part), lambda *_: (0, 0, 0)),
        ),
    )(side, *args)


def join_down_kernel(count, has_total, side_ref, own_ref, other_ref, *refs):
    firsts, seconds = refs[:count], refs[count : 2 * count]
    state_ref, out_ref, square_ref = refs[-3:]
    total = refs[2 * count][...] if has_total else jnp.zeros(out_ref.shape, F32)
    square = refs[2 * count + 1][...] if has_total else jnp.zeros(square_ref.shape, F32)
    half = own_ref.shape[-1]
    lower = side_ref[0] == 0
    for n in range(count):
        own, other = own_ref[n], other_ref[n]
        left = jnp.where(lower, own, other)
        right = jnp.where(lower, other, own)
        state_ref[n, :, :half] = left
        state_ref[n, :, half:] = right
        total += jnp.dot(left, firsts[n][...], preferred_element_type=F32)
        total += jnp.dot(right, seconds[n][...], preferred_element_type=F32)
        for x in (own.astype(F32), other.astype(F32)):
            square += jnp.sum(x * x, axis=-1, keepdims=True)
    out_ref[...] = total
    square_ref[...] = square


def join_down(before, side, own, other, firsts, seconds):
    count, rows, half = own.shape
    inner = firsts[0].shape[1]
    args = [own, other] + firsts + seconds + list(before or ())
    shapes = (
        jax.ShapeDtypeStruct((count, rows, 2 * half), BF16),
        jax.ShapeDtypeStruct((rows, inner), F32),
        jax.ShapeDtypeStruct((rows, 1), F32),
    )
    return pl.pallas_call(
        functools.partial(join_down_kernel, count, before is not None),
        out_shape=shapes,
        grid_spec=pltpu.PrefetchScalarGridSpec(
            num_scalar_prefetch=1,
            grid=(1,),
            in_specs=[whole(x) for x in args],
            out_specs=tuple(whole(x) for x in shapes),
        ),
    )(side, *args)


def finish_kernel(count, has_before, sources_ref, last_ref, active_ref, state_ref, *refs):
    firsts, seconds = refs[:count], refs[count : 2 * count]
    out_ref = refs[-1]
    half = firsts[0].shape[0]
    for n in range(count):

        @pl.when(pl.program_id(0) == n)
        def _(n=n):
            branch = jnp.dot(active_ref[:, :half], firsts[n][...], preferred_element_type=F32)
            branch += jnp.dot(active_ref[:, half:], seconds[n][...], preferred_element_type=F32)
            base = state_ref[0]
            added = (base.astype(F32) + branch).astype(BF16)
            out_ref[...] = jnp.where(last_ref[0] == 1, added, base)


def finish(before, sources, last, active, state, firsts, seconds, width):
    count, rows, part = state.shape
    args = [active, state] + firsts + seconds
    specs = [
        pl.BlockSpec(active.shape, lambda *_: (0, 0)),
        pl.BlockSpec((1, rows, part), lambda n, *_: (n, 0, 0)),
    ] + [pl.BlockSpec(x.shape, lambda *_: (0, 0)) for x in firsts + seconds]
    alias = {}
    if before is not None:
        alias = {2 + len(args): 0}
        args.append(before)
        specs.append(pl.BlockSpec(memory_space=pl.ANY))
    return pl.pallas_call(
        functools.partial(finish_kernel, count, before is not None),
        out_shape=jax.ShapeDtypeStruct((rows, width), BF16),
        grid_spec=pltpu.PrefetchScalarGridSpec(
            num_scalar_prefetch=2,
            grid=(count,),
            in_specs=specs,
            out_specs=pl.BlockSpec((rows, part), lambda n, s, _: (0, s[n])),
        ),
        input_output_aliases=alias,
    )(sources, last, *args)


def local(ring, text, image, positions, enc_in, enc_out, conn_in, conn_out, llm_in, llm_out):
    section = lax.axis_index("section")
    sections = lax.axis_size("section")
    me = lax.axis_index("dp")
    sources = lax.dynamic_index_in_dim(jnp.asarray(ring.table), me, 0, keepdims=False)
    side = section.astype(jnp.int32).reshape(1)
    last = (section == sections - 1).astype(jnp.int32).reshape(1)
    micro_count, image_count = positions.shape
    rows, width = text.shape
    image_rows, vision_width = image.shape
    slots = ring.slots
    send = lambda x, pairs: lax.ppermute(x, "section", pairs)
    onward = [(i, i + 1) for i in range(sections - 1)]

    vision_part = enc_in.shape[1]
    pack = jnp.stack([enc_in[0], enc_out[0].T])
    lanes = -(-vision_part // 128) * 128
    conn = jnp.concatenate(
        [jnp.pad(conn_in.T, ((0, 0), (0, lanes - vision_part))), conn_out], axis=1
    )
    split = llm_in.shape[1] // 2
    down_first, down_second = llm_in[0, :split], llm_in[0, split:]
    inner = llm_out.shape[1]
    column = llm_out.shape[2] // 2
    up_own = llm_out[0]
    crossed = send(up_own[:, column:], [(0, 1)])
    half = jnp.where(section == 0, up_own[:, :column], crossed)
    (packs, conns), token = ring.gather(pack, conn)
    (in_first, in_second), token = ring.gather(down_first, down_second, token)
    (half_first, half_second), token = ring.gather(half[: inner // 2], half[inner // 2 :], token)
    (out_first, out_second), token = ring.gather(up_own[: inner // 2], up_own[inner // 2 :], token)

    blocks = image.reshape(image_rows, slots, vision_part).transpose(1, 0, 2)
    hidden = jnp.take(blocks, sources, axis=0)
    for layer in range(sections - 1):
        hidden = send(encoder_layer(hidden, packs, []), onward)
    latent = encoder_layer(hidden, packs, conns)
    front = send(latent, [(sections - 1, 0)])
    if sections > 2:
        front = jnp.where(section == 0, front, send(latent, [(sections - 1, 1)]))
        latent = front
    latent = jnp.where(section == 0, front, latent)
    conn_up = jnp.stack([c[:, lanes:] for c in conns])

    row_count = rows // micro_count
    row_ids = lax.broadcasted_iota(jnp.int32, (1, row_count, 1), 1)
    matches = (positions[:, None, :] == row_ids).astype(BF16)
    same = jnp.eye(micro_count, dtype=BF16)
    place = (matches[:, :, None, :] * same[:, None, :, None]).reshape(rows, micro_count * image_count)
    state, square = merge(sources, text, place, latent, conn_up)

    def activate(total, square):
        scale = lax.rsqrt(square / width + EPSILON)
        return jax.nn.silu(total * scale).astype(BF16)

    total = None
    for group in ring.groups:
        pick = lambda xs: [xs[j] for j in group]
        total = down(total, state, group, pick(in_first), pick(in_second))
    active = activate(total, square)
    active = jnp.where(section == 0, active, send(active, [(0, 1)]))
    exchange = [(0, 1), (1, 0)]
    before, states = None, []
    for group in ring.groups:
        pick = lambda xs: [xs[j] for j in group]
        own = up_half(side, active, state, group, pick(half_first), pick(half_second))
        other = send(own, exchange)
        joined, *before = join_down(before, side, own, other, pick(in_first), pick(in_second))
        states.append(joined)

    for layer in range(1, sections):
        if layer > 1:
            before = (
                sum(
                    jnp.dot(states[g][n, :, :split], in_first[j], preferred_element_type=F32)
                    + jnp.dot(states[g][n, :, split:], in_second[j], preferred_element_type=F32)
                    for g, group in enumerate(ring.groups)
                    for n, j in enumerate(group)
                ),
                sum(
                    jnp.sum(jnp.square(x.astype(F32)), axis=(0, 2))[:, None] for x in states
                ),
            )
        active = activate(*before)
        if layer == sections - 1:
            break
        kept = states if layer == 1 else kept
        states = [
            jnp.stack(
                [
                    (
                        states[g][n].astype(F32)
                        + jnp.dot(active[:, : inner // 2], out_first[j], preferred_element_type=F32)
                        + jnp.dot(active[:, inner // 2 :], out_second[j], preferred_element_type=F32)
                    ).astype(BF16)
                    for n, j in enumerate(group)
                ]
            )
            for g, group in enumerate(ring.groups)
        ]
        kept = [jnp.where(section == layer, x, k) for x, k in zip(states, kept)]
        states = [send(x, [(layer, layer + 1)]) for x in states]
    if sections > 2:
        states = [jnp.where(section == sections - 1, x, k) for x, k in zip(states, kept)]
    out = None
    for g, group in enumerate(ring.groups):
        pick = lambda xs: [xs[j] for j in group]
        places = sources[group[0] : group[0] + len(group)]
        out = finish(out, places, last, active, states[g], pick(out_first), pick(out_second), width)
    return out[None]


def solution(mesh):
    ring = Ring(chip_cycle(mesh, mesh.shape["dp"] // 2))
    return jax.shard_map(
        functools.partial(local, ring),
        mesh=mesh,
        in_specs=(
            P("dp", None),
            P("dp", None),
            P("dp", None),
            P("section", "dp", None),
            P("section", None, "dp"),
            P("dp", None),
            P(None, "dp"),
            P("section", "dp", None),
            P("section", None, "dp"),
        ),
        out_specs=P("section", "dp", None),
        check_vma=False,
    )
```

```python
import functools

import jax
import jax.numpy as jnp
import numpy as np
from jax import lax
from jax.experimental import pallas as pl
from jax.experimental.pallas import tpu as pltpu
from jax.sharding import PartitionSpec as P

EPSILON = 1e-06
BF16 = jnp.bfloat16
F32 = jnp.float32


def chip_cycle(mesh, count):
    plain = list(range(count))
    line = mesh.devices.reshape(-1, mesh.shape["dp"])[0][::2]
    coords = [tuple(getattr(dev, "coords", (i,))) for i, dev in enumerate(line)]
    if len(set(coords)) != count:
        return plain
    varying = [a for a in range(len(coords[0])) if len({c[a] for c in coords}) > 1]
    if len(varying) != 2:
        return plain
    first, second = varying
    if len({c[first] for c in coords}) % 2:
        first, second = second, first
    rows = sorted({c[first] for c in coords})
    cols = sorted({c[second] for c in coords})
    if len(rows) % 2 or len(rows) * len(cols) != count:
        return plain
    where = {(c[first], c[second]): i for i, c in enumerate(coords)}
    path = []
    for n, row in enumerate(rows):
        walk = cols[1:] if n % 2 == 0 else cols[:0:-1]
        path += [where[row, col] for col in walk]
    return path + [where[row, cols[0]] for row in reversed(rows)]


class Ring:
    def __init__(self, cycle):
        self.cycle = cycle
        self.chips = len(cycle)
        self.reach = self.chips // 2
        self.place = {chip: i for i, chip in enumerate(cycle)}
        self.even = self.chips % 2 == 0
        self.groups = [[0]] + [[2 * k - 1, 2 * k] for k in range(1, self.reach + 1)]
        if self.even:
            self.groups[-1] = [2 * self.reach - 1]
        self.slots = self.chips
        self.table = np.array([self.sources(d) for d in range(2 * self.chips)], np.int32)

    def sources(self, device):
        chip, core = divmod(device, 2)
        at = self.place[chip]
        found = [device]
        for k in range(1, self.reach + 1):
            other = self.cycle[(at + (k if core else -k)) % self.chips]
            found += [2 * other + core, 2 * other + 1 - core]
        return found[: self.slots]

    def shift(self, x):
        pairs = []
        for i, chip in enumerate(self.cycle):
            for core in (0, 1):
                to = self.cycle[(i + (-1 if core else 1)) % self.chips]
                pairs.append((2 * chip + core, 2 * to + core))
        return lax.ppermute(x, "dp", pairs)

    def swap(self, x):
        return lax.ppermute(x, "dp", [(i, i ^ 1) for i in range(2 * self.chips)])

    def gather(self, own, after=None):
        if after is not None:
            own, _ = lax.optimization_barrier((own, after))
        got = [own]
        mine, theirs = own, self.swap(own)
        token = own
        for k in range(1, self.reach + 1):
            token = mine
            mine = self.shift(mine)
            got.append(mine)
            if not (self.even and k == self.reach):
                theirs = self.shift(theirs)
                got.append(theirs)
        return got, token


def whole(x):
    return pl.BlockSpec(x.shape, lambda *_: (0,) * len(x.shape))


def gelu(values):
    return 0.5 * values * (1.0 + lax.erf(values * np.float32(np.sqrt(0.5))))


def encoder_kernel(with_conn, hidden_ref, mine_ref, theirs_ref, out_ref):
    half = mine_ref.shape[0]
    slots = 2 * half
    width = slots * hidden_ref.shape[-1]

    def pack(j, which):
        return mine_ref[j, which] if j < half else theirs_ref[j - half, which]

    def scale_of(blocks):
        total = sum(jnp.sum(b * b, axis=-1, keepdims=True) for b in blocks)
        return lax.rsqrt(total / width + EPSILON)

    def project(blocks, which):
        scale = scale_of(blocks)
        return sum(
            jnp.dot((b * scale).astype(BF16), pack(j, which), preferred_element_type=F32)
            for j, b in enumerate(blocks)
        )

    blocks = [hidden_ref[j].astype(F32) for j in range(slots)]
    active = gelu(project(blocks, 0)).astype(BF16)
    contract = (((1,), (1,)), ((), ()))
    outs = [
        (b + lax.dot_general(active, pack(j, 1), contract, preferred_element_type=F32)).astype(BF16)
        for j, b in enumerate(blocks)
    ]
    if with_conn:
        latent = project([b.astype(F32) for b in outs], 2)
        out_ref[...] = gelu(latent[:, : out_ref.shape[-1]]).astype(BF16)
    else:
        for j in range(slots):
            out_ref[j] = outs[j]


def encoder_layer(hidden, mine, theirs, inner=None):
    shape = hidden.shape if inner is None else (hidden.shape[1], inner)
    args = [hidden, mine, theirs]
    out = jax.ShapeDtypeStruct(shape, BF16)
    return pl.pallas_call(
        functools.partial(encoder_kernel, inner is not None),
        out_shape=out,
        in_specs=[whole(x) for x in args],
        out_specs=whole(out),
        grid=(1,),
    )(*args)


def columns_kernel(sources_ref, text_ref, out_ref):
    out_ref[0] = text_ref[...]


def columns(sources, text, part):
    count, rows = sources.shape[0], text.shape[0]
    return pl.pallas_call(
        columns_kernel,
        out_shape=jax.ShapeDtypeStruct((count, rows, part), text.dtype),
        grid_spec=pltpu.PrefetchScalarGridSpec(
            num_scalar_prefetch=1,
            grid=(count,),
            in_specs=[pl.BlockSpec((rows, part), lambda j, s: (0, s[j]))],
            out_specs=pl.BlockSpec((1, rows, part), lambda j, s: (j, 0, 0)),
        ),
    )(sources, text)


def first_down_kernel(count, begun, place_ref, taken_ref, latent_ref, *refs):
    mine, theirs, weights = refs[:count], refs[count : 2 * count], refs[2 * count : 3 * count]
    state_ref, out_ref, square_ref = refs[-3:]
    rows = mine[0].shape[1]
    part = mine[0].shape[2]
    total, square = (
        (refs[3 * count][...], refs[3 * count + 1][...])
        if begun
        else (jnp.zeros(out_ref.shape, F32), jnp.zeros(square_ref.shape, F32))
    )
    place, latent = place_ref[...], latent_ref[...]
    taken = taken_ref[...] > 0.5
    for n in range(count):
        weight = weights[n]
        picture = jnp.dot(latent, weight[part:, :part], preferred_element_type=F32).astype(BF16)
        placed = jnp.dot(place, picture, preferred_element_type=F32)
        text = jnp.concatenate([mine[n][0], theirs[n][0]], axis=0)
        merged = jnp.where(taken, placed, text.astype(F32))
        state = merged.astype(BF16)
        state_ref[n] = state
        total += jnp.dot(state, weight[:part], preferred_element_type=F32)
        wide = merged * merged
        square += sum(wide[:, i : i + 128] for i in range(0, part, 128))
    out_ref[...] = total
    square_ref[...] = square


def first_down(before, group, place, taken, latent, mine, theirs, weights):
    _, rows, part = mine.shape
    inner = weights[0].shape[1]
    count = len(group)
    fixed = [place, taken, latent]
    args = fixed + [mine] * count + [theirs] * count + weights + list(before or ())
    block = [pl.BlockSpec((1, rows, part), lambda _, j=j: (j, 0, 0)) for j in group]
    shapes = (
        jax.ShapeDtypeStruct((count, 2 * rows, part), BF16),
        jax.ShapeDtypeStruct((2 * rows, inner), F32),
        jax.ShapeDtypeStruct((2 * rows, 128), F32),
    )
    return pl.pallas_call(
        functools.partial(first_down_kernel, count, before is not None),
        out_shape=shapes,
        in_specs=[whole(x) for x in fixed] + block * 2 + [whole(x) for x in args[3 + 2 * count :]],
        out_specs=tuple(whole(x) for x in shapes),
        grid=(1,),
    )(*args)


def up_half_kernel(count, section_ref, active_ref, state_ref, *refs):
    weights, out_ref = refs[:count], refs[-1]
    for n in range(count):
        branch = jnp.dot(active_ref[...], weights[n][...], preferred_element_type=F32)
        out_ref[n] = (state_ref[n].astype(F32) + branch).astype(BF16)


def up_half(side, active, state, weights):
    count, rows, _ = state.shape
    part = weights[0].shape[1]
    shape = (count, rows, part)
    return pl.pallas_call(
        functools.partial(up_half_kernel, count),
        out_shape=jax.ShapeDtypeStruct(shape, BF16),
        grid_spec=pltpu.PrefetchScalarGridSpec(
            num_scalar_prefetch=1,
            grid=(1,),
            in_specs=[whole(active), pl.BlockSpec(shape, lambda _, s: (0, 0, s[0]))]
            + [whole(x) for x in weights],
            out_specs=pl.BlockSpec(shape, lambda *_: (0, 0, 0)),
        ),
    )(side, active, state, *weights)


def join_down_kernel(count, begun, side_ref, own_ref, other_ref, *refs):
    weights = refs[:count]
    state_ref, out_ref, square_ref = refs[-3:]
    total, square = (
        (refs[count][...], refs[count + 1][...])
        if begun
        else (jnp.zeros(out_ref.shape, F32), jnp.zeros(square_ref.shape, F32))
    )
    half = own_ref.shape[-1]
    lower = side_ref[0] == 0
    for n in range(count):
        own, other = own_ref[n], other_ref[n]
        left = jnp.where(lower, own, other)
        right = jnp.where(lower, other, own)
        state_ref[n, :, :half] = left
        state_ref[n, :, half:] = right
        total += jnp.dot(left, weights[n][:half], preferred_element_type=F32)
        total += jnp.dot(right, weights[n][half : 2 * half], preferred_element_type=F32)
        for x in (own.astype(F32), other.astype(F32)):
            wide = x * x
            square += sum(wide[:, i : i + 128] for i in range(0, half, 128))
    out_ref[...] = total
    square_ref[...] = square


def join_down(before, side, own, other, weights):
    count, rows, half = own.shape
    inner = weights[0].shape[1]
    args = [own, other] + weights + list(before or ())
    shapes = (
        jax.ShapeDtypeStruct((count, rows, 2 * half), BF16),
        jax.ShapeDtypeStruct((rows, inner), F32),
        jax.ShapeDtypeStruct((rows, 128), F32),
    )
    return pl.pallas_call(
        functools.partial(join_down_kernel, count, before is not None),
        out_shape=shapes,
        grid_spec=pltpu.PrefetchScalarGridSpec(
            num_scalar_prefetch=1,
            grid=(1,),
            in_specs=[whole(x) for x in args],
            out_specs=tuple(whole(x) for x in shapes),
        ),
    )(side, *args)


def activate_kernel(width, total_ref, square_ref, other_ref, far_ref, out_ref):
    rows = total_ref.shape[0] // 2
    for low in (0, rows):
        flip = rows - low
        total = total_ref[low : low + rows] + other_ref[flip : flip + rows]
        square = square_ref[low : low + rows] + far_ref[flip : flip + rows]
        scale = lax.rsqrt(jnp.sum(square, axis=-1, keepdims=True) / width + EPSILON)
        value = total * scale
        out_ref[low : low + rows] = (value / (1.0 + jnp.exp(-value))).astype(BF16)


def activate(ring, width, total, square):
    args = [total, square, ring.swap(total), ring.swap(square)]
    out = jax.ShapeDtypeStruct(total.shape, BF16)
    return pl.pallas_call(
        functools.partial(activate_kernel, width),
        out_shape=out,
        in_specs=[whole(x) for x in args],
        out_specs=whole(out),
        grid=(1,),
    )(*args)


def finish_kernel(count, sources_ref, last_ref, active_ref, state_ref, *refs):
    weights = refs[:count]
    out_ref, send_ref = refs[-2:]
    rows = out_ref.shape[0]
    for n in range(count):

        @pl.when(pl.program_id(0) == n)
        def _(n=n):
            branch = jnp.dot(active_ref[...], weights[n][...], preferred_element_type=F32)
            base = state_ref[0]
            added = (base.astype(F32) + branch).astype(BF16)
            result = jnp.where(last_ref[0] == 1, added, base)
            out_ref[...] = result[:rows]
            send_ref[0] = result[rows:]


def finish(before, sources, last, active, state, weights, width):
    count, rows, part = state.shape
    rows //= 2
    args = [active, state] + weights
    specs = [
        pl.BlockSpec(active.shape, lambda *_: (0, 0)),
        pl.BlockSpec((1, 2 * rows, part), lambda n, *_: (n, 0, 0)),
    ] + [pl.BlockSpec(x.shape, lambda *_: (0, 0)) for x in weights]
    alias = {}
    if before is not None:
        alias = {2 + len(args): 0}
        args.append(before)
        specs.append(pl.BlockSpec(memory_space=pl.ANY))
    return pl.pallas_call(
        functools.partial(finish_kernel, count),
        out_shape=(
            jax.ShapeDtypeStruct((rows, width), BF16),
            jax.ShapeDtypeStruct((count, rows, part), BF16),
        ),
        grid_spec=pltpu.PrefetchScalarGridSpec(
            num_scalar_prefetch=2,
            grid=(count,),
            in_specs=specs,
            out_specs=(
                pl.BlockSpec((rows, part), lambda n, s, _: (0, s[n])),
                pl.BlockSpec((1, rows, part), lambda n, *_: (n, 0, 0)),
            ),
        ),
        input_output_aliases=alias,
    )(sources, last, *args)


def settle_kernel(owner, sources_ref, *refs):
    out_ref = refs[-1]
    for j, (g, n) in enumerate(owner):

        @pl.when(pl.program_id(0) == j)
        def _(g=g, n=n):
            out_ref[...] = refs[g][n]


def settle(out, sources, pieces):
    _, rows, part = pieces[0].shape
    owner = [(g, n) for g, x in enumerate(pieces) for n in range(x.shape[0])]
    return pl.pallas_call(
        functools.partial(settle_kernel, owner),
        out_shape=jax.ShapeDtypeStruct(out.shape, BF16),
        grid_spec=pltpu.PrefetchScalarGridSpec(
            num_scalar_prefetch=1,
            grid=(len(owner),),
            in_specs=[pl.BlockSpec(x.shape, lambda *_: (0, 0, 0)) for x in pieces]
            + [pl.BlockSpec(memory_space=pl.ANY)],
            out_specs=pl.BlockSpec((rows, part), lambda j, s: (0, s[j])),
        ),
        input_output_aliases={1 + len(pieces): 0},
    )(sources, *pieces, out)


def local(ring, text, image, positions, enc_in, enc_out, conn_in, conn_out, llm_in, llm_out):
    section = lax.axis_index("section")
    sections = lax.axis_size("section")
    me = lax.axis_index("dp")
    size = lax.axis_size("dp")
    table = jnp.asarray(np.stack([ring.table, ring.table[np.arange(size) ^ 1]], 1))
    sources = lax.dynamic_index_in_dim(table, me, 0, keepdims=False)
    sources, partner_sources = sources[0], sources[1]
    side = (section != 0).astype(jnp.int32).reshape(1)
    last = (section == sections - 1).astype(jnp.int32).reshape(1)
    micro_count, image_count = positions.shape
    rows, width = text.shape
    image_rows, vision_width = image.shape
    slots = ring.slots

    def send(x, pairs):
        return lax.ppermute(x, "section", pairs)

    def across(x, pairs):
        return lax.ppermute(
            x, ("section", "dp"), [(a * size + i, b * size + (i ^ 1)) for a, b in pairs for i in range(size)]
        )

    part = llm_in.shape[1]
    mine = columns(sources, text, part)
    theirs = ring.swap(columns(partner_sources, text, part))
    other_positions = ring.swap(positions)

    inner, latent_width = llm_out.shape[1], conn_in.shape[1]
    vision_part, encoder_inner = enc_in.shape[1:]
    pack = jnp.stack(
        [enc_in[0], enc_out[0].T, jnp.pad(conn_in, ((0, 0), (0, encoder_inner - latent_width)))]
    )
    column = llm_out.shape[2] // 2
    crossed = send(llm_out[0][:, column:], [(0, 1)])
    packs, _ = ring.gather(pack)
    joint_up = jnp.pad(conn_out, ((0, 0), (0, inner - conn_out.shape[1])))
    downs, token = ring.gather(jnp.concatenate([llm_in[0], joint_up], axis=0))
    half = jnp.where(section == 0, llm_out[0][:, :column], crossed)
    halves, token = ring.gather(half, token)
    ups, token = ring.gather(llm_out[0], token)

    packs = jnp.stack(packs)
    other_packs = ring.swap(packs)
    blocks = image.reshape(image_rows, size, vision_part).transpose(1, 0, 2)
    hidden = jnp.take(blocks, jnp.concatenate([sources, partner_sources]), axis=0)
    for layer in range(sections - 1):
        hidden = send(encoder_layer(hidden, packs, other_packs), [(layer, layer + 1)])
    latent = encoder_layer(hidden, packs, other_packs, latent_width)
    final = sections - 1
    own_latent = send(latent, [(final, 0)])
    other_latent = across(latent, [(final, 0)])
    if final > 1:
        front = (send(latent, [(final, 1)]), across(latent, [(final, 1)]))
    else:
        front = (latent, ring.swap(latent))
    latent = jnp.where(
        section == 0, jnp.concatenate([own_latent, other_latent]), jnp.concatenate(front)
    )

    count = 2 * micro_count
    spots = jnp.concatenate([positions, other_positions])
    row_count = rows // micro_count
    row_ids = lax.broadcasted_iota(jnp.int32, (1, row_count, 1), 1)
    matches = (spots[:, None, :] == row_ids).astype(BF16)
    same = jnp.eye(count, dtype=BF16)
    place = (matches[:, :, None, :] * same[:, None, :, None]).reshape(2 * rows, count * image_count)
    taken = jnp.any(spots[:, None, :] == row_ids, axis=-1).astype(F32).reshape(2 * rows, 1)

    before, states = None, []
    for group in ring.groups:
        pick = [downs[j] for j in group]
        state, *before = first_down(before, group, place, taken, latent, mine, theirs, pick)
        states.append(state)
    active = activate(ring, width, *before)
    active = jnp.where(section == 0, active, send(active, [(0, 1)]))
    before = None
    for g, group in enumerate(ring.groups):
        own = up_half(side, active, states[g], [halves[j] for j in group])
        other = send(own, [(0, 1), (1, 0)])
        states[g], *before = join_down(before, side, own, other, [downs[j] for j in group])

    kept = states
    for layer in range(1, sections):
        if layer > 1:
            blocks = [(states[g][n], j) for g, group in enumerate(ring.groups) for n, j in enumerate(group)]
            before = (
                sum(jnp.dot(x, downs[j][:part], preferred_element_type=F32) for x, j in blocks),
                sum(
                    jnp.sum(jnp.square(x.astype(F32)).reshape(2 * rows, -1, 128), axis=1) for x, _ in blocks
                ),
            )
        active = activate(ring, width, *before)
        if layer == final:
            break
        states = [
            jnp.stack(
                [
                    (x.astype(F32) + jnp.dot(active, ups[j], preferred_element_type=F32)).astype(BF16)
                    for x, j in zip(states[g], group)
                ]
            )
            for g, group in enumerate(ring.groups)
        ]
        kept = [jnp.where(section == layer, x, k) for x, k in zip(states, kept)]
        states = [send(x, [(layer, layer + 1)]) for x in states]
    if final > 1:
        states = [jnp.where(section == final, x, k) for x, k in zip(states, kept)]
    out, pieces = None, []
    for g, group in enumerate(ring.groups):
        places = sources[group[0] : group[0] + len(group)]
        out, piece = finish(out, places, last, active, states[g], [ups[j] for j in group], width)
        pieces.append(ring.swap(piece))
    return settle(out, partner_sources, pieces)[None]


def solution(mesh):
    ring = Ring(chip_cycle(mesh, mesh.shape["dp"] // 2))
    return jax.shard_map(
        functools.partial(local, ring),
        mesh=mesh,
        in_specs=(
            P("dp", None),
            P("dp", None),
            P("dp", None),
            P("section", "dp", None),
            P("section", None, "dp"),
            P("dp", None),
            P(None, "dp"),
            P("section", "dp", None),
            P("section", None, "dp"),
        ),
        out_specs=P("section", "dp", None),
        check_vma=False,
    )
```

```python
import functools

import jax
import jax.numpy as jnp
import numpy as np
from jax import lax
from jax.experimental import pallas as pl
from jax.experimental.pallas import tpu as pltpu
from jax.sharding import PartitionSpec as P

EPSILON = 1e-06
BF16 = jnp.bfloat16
F32 = jnp.float32


def chip_cycle(mesh, count):
    plain = list(range(count))
    line = mesh.devices.reshape(-1, mesh.shape["dp"])[0][::2]
    coords = [tuple(getattr(dev, "coords", (i,))) for i, dev in enumerate(line)]
    if len(set(coords)) != count:
        return plain
    varying = [a for a in range(len(coords[0])) if len({c[a] for c in coords}) > 1]
    if len(varying) != 2:
        return plain
    first, second = varying
    if len({c[first] for c in coords}) % 2:
        first, second = second, first
    rows = sorted({c[first] for c in coords})
    cols = sorted({c[second] for c in coords})
    if len(rows) % 2 or len(rows) * len(cols) != count:
        return plain
    where = {(c[first], c[second]): i for i, c in enumerate(coords)}
    path = []
    for n, row in enumerate(rows):
        walk = cols[1:] if n % 2 == 0 else cols[:0:-1]
        path += [where[row, col] for col in walk]
    return path + [where[row, cols[0]] for row in reversed(rows)]


class Ring:
    def __init__(self, cycle):
        self.cycle = cycle
        self.chips = len(cycle)
        self.reach = self.chips // 2
        self.place = {chip: i for i, chip in enumerate(cycle)}
        self.even = self.chips % 2 == 0
        self.groups = [[0]] + [[2 * k - 1, 2 * k] for k in range(1, self.reach + 1)]
        if self.even:
            self.groups[-1] = [2 * self.reach - 1]
        self.slots = self.chips
        self.table = np.array([self.sources(d) for d in range(2 * self.chips)], np.int32)

    def sources(self, device):
        chip, core = divmod(device, 2)
        at = self.place[chip]
        found = [device]
        for k in range(1, self.reach + 1):
            other = self.cycle[(at + (k if core else -k)) % self.chips]
            found += [2 * other + core, 2 * other + 1 - core]
        return found[: self.slots]

    def shift(self, x):
        pairs = []
        for i, chip in enumerate(self.cycle):
            for core in (0, 1):
                to = self.cycle[(i + (-1 if core else 1)) % self.chips]
                pairs.append((2 * chip + core, 2 * to + core))
        return lax.ppermute(x, "dp", pairs)

    def swap(self, x):
        return lax.ppermute(x, "dp", [(i, i ^ 1) for i in range(2 * self.chips)])

    def gather(self, own, after=None):
        if after is not None:
            own, _ = lax.optimization_barrier((own, after))
        got = [own]
        mine, theirs = own, self.swap(own)
        token = own
        for k in range(1, self.reach + 1):
            token = mine
            mine = self.shift(mine)
            got.append(mine)
            if not (self.even and k == self.reach):
                theirs = self.shift(theirs)
                got.append(theirs)
        return got, token


def whole(x):
    return pl.BlockSpec(x.shape, lambda *_: (0,) * len(x.shape))


def gelu(values):
    return 0.5 * values * (1.0 + lax.erf(values * np.float32(np.sqrt(0.5))))


def encoder_kernel(with_conn, table_ref, hidden_ref, mine_ref, theirs_ref, out_ref, pack_ref):
    half = mine_ref.shape[0]
    slots, part = 2 * half, mine_ref.shape[2]
    width = slots * part
    for j in range(half):
        pack_ref[table_ref[0, j]] = mine_ref[j]
        pack_ref[table_ref[1, j]] = theirs_ref[j]

    def project(hidden, which):
        total = jnp.sum(hidden * hidden, axis=-1, keepdims=True)
        normed = (hidden * lax.rsqrt(total / width + EPSILON)).astype(BF16)
        return sum(
            jnp.dot(normed[:, j * part : (j + 1) * part], pack_ref[j, which], preferred_element_type=F32)
            for j in range(slots)
        )

    hidden = hidden_ref[...].astype(F32)
    active = gelu(project(hidden, 0)).astype(BF16)
    contract = (((1,), (1,)), ((), ()))
    branch = jnp.concatenate(
        [
            lax.dot_general(active, pack_ref[j, 1], contract, preferred_element_type=F32)
            for j in range(slots)
        ],
        axis=1,
    )
    result = (hidden + branch).astype(BF16)
    if with_conn:
        latent = project(result.astype(F32), 2)
        out_ref[...] = gelu(latent[:, : out_ref.shape[-1]]).astype(BF16)
    else:
        out_ref[...] = result


def encoder_layer(table, hidden, mine, theirs, inner=None):
    shape = hidden.shape if inner is None else (hidden.shape[0], inner)
    args = [hidden, mine, theirs]
    out = jax.ShapeDtypeStruct(shape, BF16)
    return pl.pallas_call(
        functools.partial(encoder_kernel, inner is not None),
        out_shape=out,
        grid_spec=pltpu.PrefetchScalarGridSpec(
            num_scalar_prefetch=1,
            grid=(1,),
            in_specs=[whole(x) for x in args],
            out_specs=whole(out),
            scratch_shapes=[pltpu.VMEM((2 * mine.shape[0], *mine.shape[1:]), mine.dtype)],
        ),
    )(table, *args)


def columns_kernel(sources_ref, text_ref, after_ref, out_ref, sems):
    count, _, part = out_ref.shape
    copies = [
        pltpu.make_async_copy(
            text_ref.at[:, pl.ds(pl.multiple_of(sources_ref[j] * part, part), part)],
            out_ref.at[j],
            sems.at[j],
        )
        for j in range(count)
    ]
    for copy in copies:
        copy.start()
    for copy in copies:
        copy.wait()


def columns(sources, text, part, after):
    count, rows = sources.shape[0], text.shape[0]
    return pl.pallas_call(
        columns_kernel,
        out_shape=jax.ShapeDtypeStruct((count, rows, part), text.dtype),
        grid_spec=pltpu.PrefetchScalarGridSpec(
            num_scalar_prefetch=1,
            grid=(1,),
            in_specs=[pl.BlockSpec(memory_space=pl.ANY)] * 2,
            out_specs=pl.BlockSpec(memory_space=pl.ANY),
            scratch_shapes=[pltpu.SemaphoreType.DMA((count,))],
        ),
    )(sources, text, after)


def first_down_kernel(count, begun, sources_ref, place_ref, taken_ref, latent_ref, *refs):
    mine, theirs, weights = refs[:count], refs[count : 2 * count], refs[2 * count : 3 * count]
    state_ref, out_ref, square_ref = refs[-3:]
    part = mine[0].shape[1]
    total, square = (
        (refs[3 * count][...], refs[3 * count + 1][...])
        if begun
        else (jnp.zeros(out_ref.shape, F32), jnp.zeros(square_ref.shape, F32))
    )
    place, latent = place_ref[...], latent_ref[...]
    taken = taken_ref[...] > 0.5
    for n in range(count):
        weight = weights[n]
        picture = jnp.dot(latent, weight[part:, :part], preferred_element_type=F32).astype(BF16)
        placed = jnp.dot(place, picture, preferred_element_type=F32)
        text = jnp.concatenate([mine[n][...], theirs[n][0]], axis=0)
        merged = jnp.where(taken, placed, text.astype(F32))
        state = merged.astype(BF16)
        state_ref[n] = state
        total += jnp.dot(state, weight[:part], preferred_element_type=F32)
        wide = merged * merged
        square += sum(wide[:, i : i + 128] for i in range(0, part, 128))
    out_ref[...] = total
    square_ref[...] = square


def first_down(before, sources, group, place, taken, latent, text, theirs, weights):
    _, rows, part = theirs.shape
    inner = weights[0].shape[1]
    count = len(group)
    fixed = [place, taken, latent]
    args = fixed + [text] * count + [theirs] * count + weights + list(before or ())
    block = [pl.BlockSpec((rows, part), lambda _, s, j=j: (0, s[j])) for j in group]
    block += [pl.BlockSpec((1, rows, part), lambda _, s, j=j: (j, 0, 0)) for j in group]
    shapes = (
        jax.ShapeDtypeStruct((count, 2 * rows, part), BF16),
        jax.ShapeDtypeStruct((2 * rows, inner), F32),
        jax.ShapeDtypeStruct((2 * rows, 128), F32),
    )
    return pl.pallas_call(
        functools.partial(first_down_kernel, count, before is not None),
        out_shape=shapes,
        grid_spec=pltpu.PrefetchScalarGridSpec(
            num_scalar_prefetch=1,
            grid=(1,),
            in_specs=[whole(x) for x in fixed] + block + [whole(x) for x in args[3 + 2 * count :]],
            out_specs=tuple(whole(x) for x in shapes),
        ),
    )(sources, *args)


def up_half_kernel(count, side_ref, near_ref, far_ref, state_ref, *refs):
    weights, out_ref = refs[:count], refs[-1]
    active = jnp.where(side_ref[0] == 0, near_ref[...], far_ref[...])
    for n in range(count):
        branch = jnp.dot(active, weights[n][...], preferred_element_type=F32)
        out_ref[n] = (state_ref[n].astype(F32) + branch).astype(BF16)


def up_half(side, near, far, state, weights, after):
    count, rows, _ = state.shape
    part = weights[0].shape[1]
    shape = (count, rows, part)
    return pl.pallas_call(
        functools.partial(up_half_kernel, count),
        out_shape=jax.ShapeDtypeStruct(shape, BF16),
        grid_spec=pltpu.PrefetchScalarGridSpec(
            num_scalar_prefetch=1,
            grid=(1,),
            in_specs=[whole(near), whole(far), pl.BlockSpec(shape, lambda _, s: (0, 0, s[0]))]
            + [whole(x) for x in weights]
            + [pl.BlockSpec(memory_space=pl.ANY)],
            out_specs=pl.BlockSpec(shape, lambda *_: (0, 0, 0)),
        ),
    )(side, near, far, state, *weights, after)


def join_down_kernel(count, begun, side_ref, own_ref, other_ref, *refs):
    weights = refs[:count]
    state_ref, out_ref, square_ref = refs[-3:]
    total, square = (
        (refs[count][...], refs[count + 1][...])
        if begun
        else (jnp.zeros(out_ref.shape, F32), jnp.zeros(square_ref.shape, F32))
    )
    half = own_ref.shape[-1]
    lower = side_ref[0] == 0
    for n in range(count):
        own, other = own_ref[n], other_ref[n]
        left = jnp.where(lower, own, other)
        right = jnp.where(lower, other, own)
        state_ref[n, :, :half] = left
        state_ref[n, :, half:] = right
        total += jnp.dot(left, weights[n][:half], preferred_element_type=F32)
        total += jnp.dot(right, weights[n][half : 2 * half], preferred_element_type=F32)
        for x in (own.astype(F32), other.astype(F32)):
            wide = x * x
            square += sum(wide[:, i : i + 128] for i in range(0, half, 128))
    out_ref[...] = total
    square_ref[...] = square


def join_down(before, side, own, other, weights):
    count, rows, half = own.shape
    inner = weights[0].shape[1]
    args = [own, other] + weights + list(before or ())
    shapes = (
        jax.ShapeDtypeStruct((count, rows, 2 * half), BF16),
        jax.ShapeDtypeStruct((rows, inner), F32),
        jax.ShapeDtypeStruct((rows, 128), F32),
    )
    return pl.pallas_call(
        functools.partial(join_down_kernel, count, before is not None),
        out_shape=shapes,
        grid_spec=pltpu.PrefetchScalarGridSpec(
            num_scalar_prefetch=1,
            grid=(1,),
            in_specs=[whole(x) for x in args],
            out_specs=tuple(whole(x) for x in shapes),
        ),
    )(side, *args)


def activate_kernel(width, total_ref, square_ref, other_ref, far_ref, out_ref):
    rows = total_ref.shape[0] // 2
    for low in (0, rows):
        flip = rows - low
        total = total_ref[low : low + rows] + other_ref[flip : flip + rows]
        square = square_ref[low : low + rows] + far_ref[flip : flip + rows]
        scale = lax.rsqrt(jnp.sum(square, axis=-1, keepdims=True) / width + EPSILON)
        value = total * scale
        out_ref[low : low + rows] = (value / (1.0 + jnp.exp(-value))).astype(BF16)


def activate(ring, width, total, square):
    args = [total, square, ring.swap(total), ring.swap(square)]
    out = jax.ShapeDtypeStruct(total.shape, BF16)
    return pl.pallas_call(
        functools.partial(activate_kernel, width),
        out_shape=out,
        in_specs=[whole(x) for x in args],
        out_specs=whole(out),
        grid=(1,),
    )(*args)


def finish_kernel(count, sources_ref, last_ref, active_ref, state_ref, *refs):
    weights = refs[:count]
    out_ref, send_ref = refs[-2:]
    rows = out_ref.shape[0]
    for n in range(count):

        @pl.when(pl.program_id(0) == n)
        def _(n=n):
            branch = jnp.dot(active_ref[...], weights[n][...], preferred_element_type=F32)
            base = state_ref[0]
            added = (base.astype(F32) + branch).astype(BF16)
            result = jnp.where(last_ref[0] == 1, added, base)
            out_ref[...] = result[:rows]
            send_ref[0] = result[rows:]


def finish(before, sources, last, active, state, weights, width):
    count, rows, part = state.shape
    rows //= 2
    args = [active, state] + weights
    specs = [
        pl.BlockSpec(active.shape, lambda *_: (0, 0)),
        pl.BlockSpec((1, 2 * rows, part), lambda n, *_: (n, 0, 0)),
    ] + [pl.BlockSpec(x.shape, lambda *_: (0, 0)) for x in weights]
    alias = {}
    if before is not None:
        alias = {2 + len(args): 0}
        args.append(before)
        specs.append(pl.BlockSpec(memory_space=pl.ANY))
    return pl.pallas_call(
        functools.partial(finish_kernel, count),
        out_shape=(
            jax.ShapeDtypeStruct((rows, width), BF16),
            jax.ShapeDtypeStruct((count, rows, part), BF16),
        ),
        grid_spec=pltpu.PrefetchScalarGridSpec(
            num_scalar_prefetch=2,
            grid=(count,),
            in_specs=specs,
            out_specs=(
                pl.BlockSpec((rows, part), lambda n, s, _: (0, s[n])),
                pl.BlockSpec((1, rows, part), lambda n, *_: (n, 0, 0)),
            ),
        ),
        input_output_aliases=alias,
    )(sources, last, *args)


def settle_kernel(owner, sources_ref, *refs):
    out_ref = refs[-1]
    for j, (g, n) in enumerate(owner):

        @pl.when(pl.program_id(0) == j)
        def _(g=g, n=n):
            out_ref[...] = refs[g][n]


def settle(out, sources, pieces):
    _, rows, part = pieces[0].shape
    owner = [(g, n) for g, x in enumerate(pieces) for n in range(x.shape[0])]
    return pl.pallas_call(
        functools.partial(settle_kernel, owner),
        out_shape=jax.ShapeDtypeStruct(out.shape, BF16),
        grid_spec=pltpu.PrefetchScalarGridSpec(
            num_scalar_prefetch=1,
            grid=(len(owner),),
            in_specs=[pl.BlockSpec(x.shape, lambda *_: (0, 0, 0)) for x in pieces]
            + [pl.BlockSpec(memory_space=pl.ANY)],
            out_specs=pl.BlockSpec((rows, part), lambda j, s: (0, s[j])),
        ),
        input_output_aliases={1 + len(pieces): 0},
    )(sources, *pieces, out)


def local(ring, text, image, positions, enc_in, enc_out, conn_in, conn_out, llm_in, llm_out):
    section = lax.axis_index("section")
    sections = lax.axis_size("section")
    me = lax.axis_index("dp")
    size = lax.axis_size("dp")
    table = jnp.asarray(np.stack([ring.table, ring.table[np.arange(size) ^ 1]], 1))
    both_sources = lax.dynamic_index_in_dim(table, me, 0, keepdims=False)
    sources, partner_sources = both_sources[0], both_sources[1]
    side = (section != 0).astype(jnp.int32).reshape(1)
    last = (section == sections - 1).astype(jnp.int32).reshape(1)
    micro_count, image_count = positions.shape
    rows, width = text.shape
    image_rows, vision_width = image.shape
    slots = ring.slots

    def send(x, pairs):
        return lax.ppermute(x, "section", pairs)

    def across(x, pairs):
        return lax.ppermute(
            x, ("section", "dp"), [(a * size + i, b * size + (i ^ 1)) for a, b in pairs for i in range(size)]
        )

    part = llm_in.shape[1]
    other_positions = ring.swap(positions)

    inner, latent_width = llm_out.shape[1], conn_in.shape[1]
    vision_part, encoder_inner = enc_in.shape[1:]
    pack = jnp.stack(
        [enc_in[0], enc_out[0].T, jnp.pad(conn_in, ((0, 0), (0, encoder_inner - latent_width)))]
    )
    column = llm_out.shape[2] // 2
    crossed = send(llm_out[0][:, column:], [(0, 1)])
    packs, _ = ring.gather(pack)
    joint_up = jnp.pad(conn_out, ((0, 0), (0, inner - conn_out.shape[1])))
    downs, token = ring.gather(jnp.concatenate([llm_in[0], joint_up], axis=0))
    half = jnp.where(section == 0, llm_out[0][:, :column], crossed)
    halves, token = ring.gather(half, token)
    ups, token = ring.gather(llm_out[0], token)

    packs = jnp.stack(packs)
    other_packs = ring.swap(packs)
    hidden = image
    for layer in range(sections - 1):
        hidden = encoder_layer(both_sources, hidden, packs, other_packs)
        if layer == 0:
            theirs = ring.swap(columns(partner_sources, text, part, hidden))
        hidden = send(hidden, [(layer, layer + 1)])
    latent = encoder_layer(both_sources, hidden, packs, other_packs, latent_width)
    final = sections - 1
    own_latent = send(latent, [(final, 0)])
    other_latent = across(latent, [(final, 0)])
    if final > 1:
        front = (send(latent, [(final, 1)]), across(latent, [(final, 1)]))
    else:
        front = (latent, ring.swap(latent))
    latent = jnp.where(
        section == 0, jnp.concatenate([own_latent, other_latent]), jnp.concatenate(front)
    )

    count = 2 * micro_count
    spots = jnp.concatenate([positions, other_positions])
    row_count = rows // micro_count
    row_ids = lax.broadcasted_iota(jnp.int32, (1, row_count, 1), 1)
    matches = (spots[:, None, :] == row_ids).astype(BF16)
    same = jnp.eye(count, dtype=BF16)
    place = (matches[:, :, None, :] * same[:, None, :, None]).reshape(2 * rows, count * image_count)
    taken = jnp.any(spots[:, None, :] == row_ids, axis=-1).astype(F32).reshape(2 * rows, 1)

    before, states = None, []
    for group in ring.groups:
        pick = [downs[j] for j in group]
        state, *before = first_down(before, sources, group, place, taken, latent, text, theirs, pick)
        states.append(state)
    active = activate(ring, width, *before)
    relayed = send(active, [(0, 1)])
    before, own = None, side
    for g, group in enumerate(ring.groups):
        own = up_half(side, active, relayed, states[g], [halves[j] for j in group], own)
        other = send(own, [(0, 1), (1, 0)])
        states[g], *before = join_down(before, side, own, other, [downs[j] for j in group])

    kept = states
    for layer in range(1, sections):
        if layer > 1:
            blocks = [(states[g][n], j) for g, group in enumerate(ring.groups) for n, j in enumerate(group)]
            before = (
                sum(jnp.dot(x, downs[j][:part], preferred_element_type=F32) for x, j in blocks),
                sum(
                    jnp.sum(jnp.square(x.astype(F32)).reshape(2 * rows, -1, 128), axis=1) for x, _ in blocks
                ),
            )
        active = activate(ring, width, *before)
        if layer == final:
            break
        states = [
            jnp.stack(
                [
                    (x.astype(F32) + jnp.dot(active, ups[j], preferred_element_type=F32)).astype(BF16)
                    for x, j in zip(states[g], group)
                ]
            )
            for g, group in enumerate(ring.groups)
        ]
        kept = [jnp.where(section == layer, x, k) for x, k in zip(states, kept)]
        states = [send(x, [(layer, layer + 1)]) for x in states]
    if final > 1:
        states = [jnp.where(section == final, x, k) for x, k in zip(states, kept)]
    out, pieces = None, []
    for g, group in enumerate(ring.groups):
        places = sources[group[0] : group[0] + len(group)]
        out, piece = finish(out, places, last, active, states[g], [ups[j] for j in group], width)
        pieces.append(ring.swap(piece))
    return settle(out, partner_sources, pieces)[None]


def solution(mesh):
    ring = Ring(chip_cycle(mesh, mesh.shape["dp"] // 2))
    return jax.shard_map(
        functools.partial(local, ring),
        mesh=mesh,
        in_specs=(
            P("dp", None),
            P("dp", None),
            P("dp", None),
            P("section", "dp", None),
            P("section", None, "dp"),
            P("dp", None),
            P(None, "dp"),
            P("section", "dp", None),
            P("section", None, "dp"),
        ),
        out_specs=P("section", "dp", None),
        check_vma=False,
    )
```
